32 devices in a mesh: groups: 2 (over y), row: 4 (over z), col: 4 (over x, core).
Axes of the slice: x: 2, y: 2, z: 4, core: 2. Of those that a mesh axis runs over, the one named last changes fastest.
Arguments:
- left_act: float32 [256, 32, 32], P(('groups', 'row'), 'col'), parts along dimension 0, may hold values from -6 to 6
- right_act: float32 [256, 32, 32], P(('groups', 'row'), 'col'), parts along dimension 0, may hold values from -6 to 6
- weight: float32 [1024, 128], replicated, may hold values from -0.75 to 0.75
- bias: float32 [128], replicated, may hold values from -1.8 to 1.8
- cotangent: float32 [64, 32, 128], P(('groups', 'row'), 'col'), parts along dimension 0, may hold values from -0.6 to 0.6
Outputs:
- pair: float32 [64, 32, 128], P(('groups', 'row'), 'col'), parts along dimension 0
- grad_left: float32 [256, 32, 32], P(('groups', 'row'), 'col'), parts along dimension 0
- grad_right: float32 [256, 32, 32], P(('groups', 'row'), 'col'), parts along dimension 0
- grad_weight: float32 [2048, 128], P(('groups', 'row')), parts along dimension 0
The draws below stay inside these ranges and needn't reach their ends.
There are 2 independent parts, one for each index of `groups`. The reference program is written for one: setup_inputs(seed, part) draws one part's arguments, and reference() takes and returns one part's arrays. A program takes and returns all parts, laid end to end along the dimension named above; an argument that names none is the same for every part. Nothing has to cross between parts.
All inputs are finite; a program needn't handle non-finite values.
Results may differ from the reference program's by a relative error of at most 0.0003.
Values sent between devices are 32-bit elements; how exact they have to be, the bound alone decides.
No kernel may reach another device: no remote copies, remote signals or barrier semaphores. Data moves between devices by JAX's collectives and lax.ppermute only.
A program may use at most 64 MiB of HBM per device.

```python
import math
import jax
import jax.numpy as jnp
from jax import lax

C = 32
Z = 128
S = 128
R = 32


def block_scale(stream_key, extent, pieces, least, high):
    loudness = 1.0
    for position, blocks in pieces:
        steps = jax.random.uniform(jax.random.fold_in(jax.random.fold_in(stream_key, 6), position), (blocks,), jnp.float32, least / len(pieces), high / len(pieces))
        loudness = loudness * jnp.repeat(jnp.exp(steps), extent[position] // blocks).reshape((-1,) + (1,) * (len(extent) - 1 - position))
    return loudness


def centred(rng, extent, scale, bound, shards=(), kind=jnp.bfloat16):
    values = scale * jax.random.normal(rng, extent, jnp.float32)
    if shards:
        values = values * block_scale(rng, extent, shards, -0.22, 0.18)
    return jnp.clip(values, -bound, bound).astype(kind)


def setup_inputs(seed: int = 0, part: int = 0) -> dict:
    keys = jax.random.split(jax.random.key(seed), 6)
    part_splits = jax.random.split(jax.random.fold_in(keys[5], part), 6)
    left_act = centred(part_splits[0], (S, R, C), 1.0, 6.0, ((0, 4), (1, 4)), jnp.float32)
    right_act = centred(part_splits[1], (S, R, C), 1.0, 6.0, ((0, 4), (1, 4)), jnp.float32)
    weight = centred(keys[2], (C * C, Z), (C * C // 16) ** -0.5, 0.75, (), jnp.float32)
    bias = centred(keys[3], (Z,), 0.3, 1.8, (), jnp.float32)
    cotangent = centred(part_splits[4], (R, R, Z), 0.1, 0.6, ((0, 4), (1, 4)), jnp.float32)
    return {"left_act": left_act, "right_act": right_act, "weight": weight, "bias": bias, "cotangent": cotangent}


def block_terms(left_block, right_full, cot_block, weight_cube, bias):
    seqs = right_full.shape[0]
    highest = lax.Precision.HIGHEST
    products = jnp.einsum("sic,sjd->icjd", left_block, right_full, precision=highest) / seqs
    pair_block = jnp.einsum("icjd,cdz->ijz", products, weight_cube, precision=highest) + bias
    grad_outer = jnp.einsum("ijz,cdz->icjd", cot_block, weight_cube, precision=highest)
    weight_term = jnp.einsum("icjd,ijz->cdz", products, cot_block, precision=highest)
    left_term = jnp.einsum("icjd,sjd->sic", grad_outer, right_full, precision=highest) / seqs
    right_term = jnp.einsum("icjd,sic->sjd", grad_outer, left_block, precision=highest) / seqs
    return pair_block, weight_term, left_term, right_term


def reference(left_act, right_act, weight, bias, cotangent):
    residues = left_act.shape[1]
    width = left_act.shape[2]
    pair_width = weight.shape[1]
    block_rows = math.gcd(residues, 32)
    block_count = residues // block_rows
    weight_cube = weight.reshape(width, width, pair_width)

    def one_block(totals, block_index):
        start = (block_index * block_rows).astype(jnp.int32)
        left_block = lax.dynamic_slice_in_dim(left_act, start, block_rows, 1)
        cot_block = lax.dynamic_slice_in_dim(cotangent, start, block_rows, 0)
        pair_block, weight_term, left_term, right_term = block_terms(left_block, right_act, cot_block, weight_cube, bias)
        return (totals[0] + weight_term, totals[1] + right_term), (pair_block, left_term)

    initial = (jnp.zeros((width, width, pair_width), jnp.float32), jnp.zeros(right_act.shape, jnp.float32))
    (grad_cube, grad_right), (pair_blocks, left_blocks) = lax.scan(one_block, initial, jnp.arange(block_count, dtype=jnp.int32))
    pair = pair_blocks.reshape(residues, residues, pair_width)
    grad_left = jnp.transpose(left_blocks, (1, 0, 2, 3)).reshape(left_act.shape)
    return pair, grad_left, grad_right, grad_cube.reshape(width * width, pair_width)
```

```python
import functools

import jax
import jax.numpy as jnp
from jax import lax
from jax.experimental import pallas as pl
from jax.experimental.pallas import tpu as pltpu
from jax.sharding import PartitionSpec as P

LANES, SUBLANES = 128, 8
NT = (((1,), (1,)), ((), ()))
NN = (((1,), (0,)), ((), ()))
TN = (((0,), (0,)), ((), ()))
TT = (((0,), (1,)), ((), ()))


def block_terms(left_block, right_full, cot_block, weight_cube, bias):
    seqs = right_full.shape[0]
    highest = lax.Precision.HIGHEST
    products = jnp.einsum("sic,sjd->icjd", left_block, right_full, precision=highest) / seqs
    pair_block = jnp.einsum("icjd,cdz->ijz", products, weight_cube, precision=highest) + bias
    grad_outer = jnp.einsum("ijz,cdz->icjd", cot_block, weight_cube, precision=highest)
    weight_term = jnp.einsum("icjd,ijz->cdz", products, cot_block, precision=highest)
    left_term = jnp.einsum("icjd,sjd->sic", grad_outer, right_full, precision=highest) / seqs
    right_term = jnp.einsum("icjd,sic->sjd", grad_outer, left_block, precision=highest) / seqs
    return (pair_block, weight_term, left_term, right_term)


def shards_general(left_act, right_act, weight, bias, cotangent):
    right_count = left_act.shape[1]
    width = left_act.shape[2]
    left_count = cotangent.shape[0]
    pair_width = weight.shape[1]
    widened = lax.all_gather(left_act, "col", axis=1, tiled=True)
    left_full = lax.all_to_all(widened, "row", split_axis=1, concat_axis=0, tiled=True)
    right_full = lax.all_gather(right_act, "row", axis=0, tiled=True)
    weight_cube = weight.reshape(width, width, pair_width)
    pair, grad_cube, left_partial, right_partial = block_terms(
        left_full, right_full, cotangent, weight_cube, bias
    )
    returned = lax.all_to_all(left_partial, "row", split_axis=0, concat_axis=1, tiled=True)
    grad_left = lax.psum_scatter(returned, "col", scatter_dimension=1, tiled=True)
    grad_right = lax.psum_scatter(right_partial, "row", scatter_dimension=0, tiled=True)
    grad_flat = grad_cube.reshape(width * width, pair_width)
    weight_part = lax.psum_scatter(grad_flat, "row", scatter_dimension=0, tiled=True)
    grad_weight = lax.psum(weight_part, "col")
    return (pair, grad_left, grad_right, grad_weight)


def split(x):
    hi = x.astype(jnp.bfloat16)
    return hi, (x - hi.astype(jnp.float32)).astype(jnp.bfloat16)


def dot3(a, b, dims):
    dot = functools.partial(lax.dot_general, dimension_numbers=dims, preferred_element_type=jnp.float32)
    (ah, al), (bh, bl) = a, b
    return dot(ah, bh) + (dot(ah, bl) + dot(al, bh))


def lane(x, block, width):
    return x[:, block * width : (block + 1) * width]


def pack_kernel(n, left, right, cot, lt, rc):
    seqs, res, width = left.shape
    share = width // n
    flat = jnp.concatenate([left[:, i, :] for i in range(res)], axis=1)
    turned = jnp.transpose(flat)
    for i in range(res):
        rows = [turned[(i * n + b) * share : (i * n + b + 1) * share] for b in range(n)]
        lt[i * share : (i + 1) * share] = jnp.concatenate(rows, axis=1)
    per = LANES // width
    tiles = res // per
    for t in range(tiles):
        rc[t * seqs : (t + 1) * seqs] = jnp.concatenate(
            [right[:, t * per + j, :] for j in range(per)], axis=1
        )
    base = tiles * seqs
    for j in range(cot.shape[1]):
        rc[base + j * res : base + (j + 1) * res] = cot[:, j, :]


def slice_kernel(n, l0, l1, l2, l3, p0, p1, p2, p3, held, built):
    r, k = lax.axis_index("row"), lax.axis_index("col")
    rows = l0.shape[0]
    wide = LANES // n
    for m, ref in enumerate((l0, l1, l2, l3)):
        held[k ^ m] = ref[...]
    owner = lax.broadcasted_iota(jnp.int32, (rows, LANES), 1) // wide
    for dest in range(n):
        out = None
        for b in range(n):
            block = held[b]
            shift = ((b - dest) * wide) % LANES
            if shift:
                block = pltpu.roll(block, shift, 1)
            out = block if out is None else jnp.where(owner == b, block, out)
        built[dest] = out
    for m, ref in enumerate((p0, p1, p2, p3)):
        ref[:rows] = held[r ^ m]
        ref[rows:] = built[r ^ m]


def gather_cot(n, rcs, cot, base, res):
    r = lax.axis_index("row")
    for m, ref in enumerate(rcs):
        for j in range(res):
            cot[j, pl.ds(pl.multiple_of((r ^ m) * res, res), res), :] = ref[base + j * res : base + (j + 1) * res]


def grads_kernel(n, seqs_all, l0, l1, l2, l3, r0, r1, r2, r3, weight, grad_right, keep, send, held, cot, inner, pieces):
    k = lax.axis_index("col")
    seqs, res, width = grad_right.shape
    share = width // n
    wide = LANES // n
    total = n * res
    tiles = res * width // LANES
    base = tiles * seqs
    for m, ref in enumerate((l0, l1, l2, l3)):
        held[pl.ds((k ^ m) * res * share, res * share)] = ref[...]
    gather_cot(n, (r0, r1, r2, r3), cot, base, res)
    cots = split(cot[...].reshape(res * total, LANES))
    inner[...] = dot3(cots, split(weight[...]), NT)
    turned = jnp.concatenate(
        [
            jnp.concatenate(
                [inner[j * total : (j + 1) * total, c * width : (c + 1) * width] for j in range(res)], axis=1
            )
            for c in range(width)
        ],
        axis=0,
    )
    g = split(turned * (1.0 / seqs_all))
    by_share = [held[pl.ds(e, total, stride=share), :] for e in range(share)]
    left = jnp.concatenate([lane(by_share[c % share], c // share, wide) for c in range(width)], axis=0)
    gr = dot3(split(left), g, TN)
    for j in range(res):
        grad_right[:, j, :] = lane(gr, j, width)
    own = jnp.concatenate([r0[t * seqs : (t + 1) * seqs] for t in range(tiles)], axis=1)
    gl = dot3(g, split(own), NT)
    for b in range(n):
        for e in range(share):
            parts = []
            for cb in range(n):
                row = ((cb * share + e) * n + b) * res
                parts.append(gl[row : row + res])
            pieces[b, e * res : (e + 1) * res] = jnp.concatenate(parts, axis=1)
    half = res * share
    keep[:half] = pieces[k]
    keep[half:] = pieces[k ^ 2]
    send[:half] = pieces[k ^ 1]
    send[half:] = pieces[k ^ 3]


def outer_kernel(n, r0, r1, r2, r3, q0, q1, q2, q3, weight, bias, pair, part, cot):
    res, _, pair_width = pair.shape
    share = SUBLANES
    width = LANES // n
    wide = LANES // n
    seqs = LANES // n
    total = n * res
    tiles = res * width // LANES
    base = tiles * seqs
    rows = res * share
    gather_cot(n, (r0, r1, r2, r3), cot, base, res)
    rights = jnp.concatenate(
        [
            jnp.concatenate([ref[t * seqs : (t + 1) * seqs] for t in range(tiles)], axis=1)
            for ref in (r0, r1, r2, r3)
        ],
        axis=0,
    )
    scaled = split(rights * (1.0 / (n * seqs)))
    qs = (q0, q1, q2, q3)

    def turn(offset):
        out = {}
        for e in range(share):
            regs = [q[pl.ds(offset + e, res, stride=share), :] for q in qs]
            for b in range(n):
                out[e, b] = jnp.concatenate([lane(reg, b, wide) for reg in regs], axis=1)
        return out

    mine = turn(0)
    lefts = jnp.concatenate([mine[c % share, c // share] for c in range(width)], axis=0)
    outer = dot3(split(lefts), scaled, NN)
    wide_rows = jnp.concatenate(
        [
            jnp.concatenate([lane(outer[c * res : (c + 1) * res], j, width) for c in range(width)], axis=1)
            for j in range(res)
        ],
        axis=0,
    )
    product = dot3(split(wide_rows), split(weight[...]), NN) + bias[...]
    for j in range(res):
        pair[:, j, :] = product[j * res : (j + 1) * res]
    theirs = turn(rows)
    shares = jnp.concatenate([theirs[e, b] for e in range(share) for b in range(n)], axis=0)
    turned = dot3(scaled, split(shares), TT)
    stacked = jnp.concatenate(
        [
            jnp.concatenate([lane(turned[j * width : (j + 1) * width], e, total) for j in range(res)], axis=1)
            for e in range(share)
        ],
        axis=0,
    )
    part[...] = dot3(split(stacked), split(cot[...].reshape(res * total, pair_width)), NN)


def middle_kernel(part, part_in, keep, gl_in, out, own):
    rows, half = part.shape[0], keep.shape[0] // 2
    out[:rows] = part[...] + part_in[...]
    out[rows:] = keep[half:] + gl_in[half:]
    own[...] = keep[:half] + gl_in[:half]


def last_kernel(n, sums, own, theirs, grad_left, grad_weight):
    rows = grad_weight.shape[0]
    seqs, res, width = grad_left.shape
    share = width // n
    grad_weight[...] = sums[:rows] + theirs[:rows]
    total = own[...] + theirs[rows:]
    for i in range(res):
        picked = jnp.concatenate([total[e * res + i : e * res + i + 1] for e in range(share)], axis=0)
        stacked = jnp.concatenate([lane(picked, cb, seqs) for cb in range(n)], axis=0)
        grad_left[:, i, :] = jnp.transpose(stacked)


def swap(x, axis, n, m):
    return lax.ppermute(x, axis, [(a, a ^ m) for a in range(n)])


def shards_packed(n, left_act, right_act, weight, bias, cotangent):
    f32 = jnp.float32
    seqs, res, width = left_act.shape
    pair_width = weight.shape[1]
    rows = seqs * res * width // LANES
    total = n * res
    vmem = pl.BlockSpec(memory_space=pltpu.VMEM)
    shape = lambda *dims: jax.ShapeDtypeStruct(dims, f32)

    def call(kernel, outs, scratch, *args):
        return pl.pallas_call(
            kernel,
            out_shape=outs,
            in_specs=[vmem] * len(args),
            out_specs=jax.tree.map(lambda _: vmem, outs),
            scratch_shapes=scratch,
        )(*args)

    packed = (shape(rows, LANES), shape(2 * rows, LANES))
    lt, rc = call(functools.partial(pack_kernel, n), packed, [], left_act, right_act, cotangent)
    lt_x = swap(lt, "col", n, 2)
    rcs = [rc] + [swap(rc, "row", n, m) for m in (1, 2, 3)]
    lt_c = swap(lt, "col", n, 1)
    lt_xc = swap(lt_x, "col", n, 1)
    lts = (lt, lt_c, lt_x, lt_xc)
    cut = call(
        functools.partial(slice_kernel, n),
        (shape(2 * rows, LANES),) * n,
        [pltpu.VMEM((n, rows, LANES), f32)] * 2,
        *lts,
    )
    qs = [cut[0]] + [swap(cut[m], "row", n, m) for m in (1, 2, 3)]
    cot_scratch = pltpu.VMEM((res, total, pair_width), f32)
    grad_right, keep, send = call(
        functools.partial(grads_kernel, n, n * seqs),
        (shape(seqs, res, width), shape(2 * rows, LANES), shape(2 * rows, LANES)),
        [
            pltpu.VMEM((n * rows, LANES), f32),
            cot_scratch,
            pltpu.VMEM((res * total, width * width), f32),
            pltpu.VMEM((n, rows, LANES), f32),
        ],
        *lts,
        *rcs,
        weight,
    )
    gl_in = swap(send, "col", n, 1)
    own_rows = width * width // n
    pair, part = call(
        functools.partial(outer_kernel, n),
        (shape(res, res, pair_width), shape(own_rows, pair_width)),
        [cot_scratch],
        *rcs,
        *qs,
        weight,
        bias.reshape(1, -1),
    )
    part_in = swap(part, "col", n, 1)
    sums, own = call(
        middle_kernel, (shape(own_rows + rows, LANES), shape(rows, LANES)), [], part, part_in, keep, gl_in
    )
    sums_in = swap(sums, "col", n, 2)
    grad_left, grad_weight = call(
        functools.partial(last_kernel, n),
        (shape(seqs, res, width), shape(own_rows, pair_width)),
        [],
        sums,
        own,
        sums_in,
    )
    return (pair, grad_left, grad_right, grad_weight)


def packs(mesh, n, left_act, weight, cotangent):
    seqs, res, width = left_act.shape
    return (
        n == 4
        and mesh.shape["col"] == n
        and cotangent.shape[:2] == (res, res)
        and n * seqs == n * width == weight.shape[1] == LANES
        and res == width // n == SUBLANES
    )


def solution(mesh):
    placed = (
        P(("groups", "row"), "col", None),
        P(("groups", "row"), "col", None),
        P(),
        P(),
        P(("groups", "row"), "col", None),
    )
    n = mesh.shape["row"]

    def shards(left_act, right_act, weight, bias, cotangent):
        if packs(mesh, n, left_act, weight, cotangent):
            return shards_packed(n, left_act, right_act, weight, bias, cotangent)
        return shards_general(left_act, right_act, weight, bias, cotangent)

    return jax.shard_map(
        shards,
        mesh=mesh,
        in_specs=placed,
        out_specs=(
            P(("groups", "row"), "col", None),
            P(("groups", "row"), "col", None),
            P(("groups", "row"), "col", None),
            P(("groups", "row"), None),
        ),
        check_vma=False,
    )
```

```python
import functools

import jax
import jax.numpy as jnp
from jax import lax
from jax.experimental import pallas as pl
from jax.experimental.pallas import tpu as pltpu
from jax.sharding import PartitionSpec as P


LANES, SUBLANES = 128, 8
NT = (((1,), (1,)), ((), ()))
NN = (((1,), (0,)), ((), ()))
TT = (((0,), (1,)), ((), ()))


def block_terms(left_block, right_full, cot_block, weight_cube, bias):
    seqs = right_full.shape[0]
    highest = lax.Precision.HIGHEST
    products = jnp.einsum("sic,sjd->icjd", left_block, right_full, precision=highest) / seqs
    pair_block = jnp.einsum("icjd,cdz->ijz", products, weight_cube, precision=highest) + bias
    grad_outer = jnp.einsum("ijz,cdz->icjd", cot_block, weight_cube, precision=highest)
    weight_term = jnp.einsum("icjd,ijz->cdz", products, cot_block, precision=highest)
    left_term = jnp.einsum("icjd,sjd->sic", grad_outer, right_full, precision=highest) / seqs
    right_term = jnp.einsum("icjd,sic->sjd", grad_outer, left_block, precision=highest) / seqs
    return (pair_block, weight_term, left_term, right_term)


def shards_general(left_act, right_act, weight, bias, cotangent):
    width = left_act.shape[2]
    pair_width = weight.shape[1]
    widened = lax.all_gather(left_act, "col", axis=1, tiled=True)
    left_full = lax.all_to_all(widened, "row", split_axis=1, concat_axis=0, tiled=True)
    right_full = lax.all_gather(right_act, "row", axis=0, tiled=True)
    weight_cube = weight.reshape(width, width, pair_width)
    pair, grad_cube, left_partial, right_partial = block_terms(
        left_full, right_full, cotangent, weight_cube, bias
    )
    returned = lax.all_to_all(left_partial, "row", split_axis=0, concat_axis=1, tiled=True)
    grad_left = lax.psum_scatter(returned, "col", scatter_dimension=1, tiled=True)
    grad_right = lax.psum_scatter(right_partial, "row", scatter_dimension=0, tiled=True)
    grad_flat = grad_cube.reshape(width * width, pair_width)
    weight_part = lax.psum_scatter(grad_flat, "row", scatter_dimension=0, tiled=True)
    grad_weight = lax.psum(weight_part, "col")
    return (pair, grad_left, grad_right, grad_weight)


def split(x):
    hi = x.astype(jnp.bfloat16)
    return hi, (x - hi.astype(jnp.float32)).astype(jnp.bfloat16)


def dot3(a, b, dims):
    dot = functools.partial(lax.dot_general, dimension_numbers=dims, preferred_element_type=jnp.float32)
    (ah, al), (bh, bl) = a, b
    (ka,), (kb,) = dims[0]
    if ah.shape[ka] <= LANES:
        return dot(jnp.concatenate([ah, al], ka), jnp.concatenate([bh, bh], kb)) + dot(ah, bl)
    width = bh.shape[1 - kb]
    if width == LANES:
        both = dot(ah, jnp.concatenate([bh, bl], 1 - kb))
        return (both[:, :width] + both[:, width:]) + dot(al, bh)
    return dot(ah, bh) + (dot(ah, bl) + dot(al, bh))


def lane(x, block, width):
    return x[:, block * width : (block + 1) * width]


def pack_kernel(n, left, right, cot, weight, bias, lt, rc, own, weight_out, bias_out, lv, rv, cv, sem):
    seqs, res, width = lv.shape
    part = seqs // n
    moves = [(left.at[pl.ds(b * part, part)], lv.at[pl.ds(b * part, part)]) for b in range(n)]
    moves += [(right.at[pl.ds(b * part, part)], rv.at[pl.ds(b * part, part)]) for b in range(n)]
    moves += [(cot, cv), (weight, weight_out), (bias, bias_out)]
    copies = [pltpu.make_async_copy(a, b, sem.at[i]) for i, (a, b) in enumerate(moves)]
    for copy in copies:
        copy.start()
    share = width // n
    for copy in copies[:n]:
        copy.wait()
    flat = jnp.concatenate([lv[:, i, :] for i in range(res)], axis=1)
    turned = jnp.transpose(flat)
    for i in range(res):
        rows = [turned[(i * n + b) * share : (i * n + b + 1) * share] for b in range(n)]
        block = jnp.concatenate(rows, axis=1)
        lt[i * share : (i + 1) * share] = block
        own[i * share : (i + 1) * share] = block
    per = LANES // width
    tiles = res // per
    base = tiles * seqs
    skip = lt.shape[0]
    for copy in copies[n : 2 * n + 1]:
        copy.wait()
    for t in range(tiles):
        block = jnp.concatenate([rv[:, t * per + j, :] for j in range(per)], axis=1)
        rc[t * seqs : (t + 1) * seqs] = block
        own[skip + t * seqs : skip + (t + 1) * seqs] = block
    for j in range(cv.shape[1]):
        block = cv[:, j, :]
        rc[base + j * res : base + (j + 1) * res] = block
        own[skip + base + j * res : skip + base + (j + 1) * res] = block
    for copy in copies[2 * n + 1 :]:
        copy.wait()


def join_kernel(lt, rc, own_x, lefts, others):
    rows = lt.shape[0]
    lefts[:rows] = lt[...]
    lefts[rows:] = own_x[:rows]
    others[: 2 * rows] = rc[...]
    others[2 * rows :] = own_x[rows:]


def halves(near, far):
    rows = near.shape[0] // 2
    return near.at[:rows], far.at[:rows], near.at[rows:], far.at[rows:]


def slice_kernel(n, near, far, p0, p1, p2, p3, both):
    r, k = lax.axis_index("row"), lax.axis_index("col")
    rows = near.shape[0] // 2
    wide = LANES // n
    for m, ref in enumerate(halves(near, far)):
        both[0, k ^ m] = ref[...]
    owner = lax.broadcasted_iota(jnp.int32, (rows, LANES), 1) // wide
    for dest in range(n):
        out = None
        for b in range(n):
            block = both[0, b]
            shift = ((b - dest) * wide) % LANES
            if shift:
                block = pltpu.roll(block, shift, 1)
            out = block if out is None else jnp.where(owner == b, block, out)
        both[1, dest] = out
    for m, ref in enumerate((p0, p1, p2, p3)):
        ref[...] = both[k & 1, r ^ m]


def chosen(n, kind, mine, theirs, both):
    odd = lax.axis_index("col") & 1
    rows = mine.shape[0] // n
    both[odd] = mine[...]
    both[1 - odd] = theirs[...]
    return [both.at[kind, m * rows : (m + 1) * rows] for m in range(n)]


def stack_kernel(*refs):
    *blocks, out = refs
    rows = blocks[0].shape[0]
    for m, ref in enumerate(blocks):
        out[m * rows : (m + 1) * rows] = ref[...]


def gather_cot(rcs, cot, base, res):
    r = lax.axis_index("row")
    for m, ref in enumerate(rcs):
        for j in range(res):
            cot[j, pl.ds(pl.multiple_of((r ^ m) * res, res), res), :] = ref[base + j * res : base + (j + 1) * res]


def grads_kernel(n, seqs_all, near, far, r0, r1, r2, r3, weight, grad_right, keep, send, held, cot, pieces):
    k = lax.axis_index("col")
    seqs, res = grad_right.shape[0], SUBLANES
    width = grad_right.shape[1] // res
    share = width // n
    wide = LANES // n
    total = n * res
    tiles = res * width // LANES
    base = tiles * seqs
    for m, ref in enumerate(halves(near, far)):
        held[pl.ds((k ^ m) * res * share, res * share)] = ref[...]
    gather_cot((r0, r1, r2, r3), cot, base, res)
    cots = split(cot[...].reshape(res * total, LANES))
    by_share = [held[pl.ds(e, total, stride=share), :] for e in range(share)]
    per = LANES // total
    turns = [jnp.transpose(jnp.concatenate(by_share[e : e + per], axis=0)) for e in range(0, share, per)]
    lefts = [
        split(jnp.concatenate([turn_[cb * wide : (cb + 1) * wide] for turn_ in turns], axis=1)) for cb in range(n)
    ]
    own = split(jnp.concatenate([r0[t * seqs : (t + 1) * seqs] for t in range(tiles)], axis=1))
    blank = jnp.zeros_like(own[0])
    lanes = share * width
    parts = []
    for cb in range(n):
        inner = dot3(cots, split(weight[cb * lanes : (cb + 1) * lanes]), NT)
        turned = jnp.concatenate(
            [
                jnp.concatenate([lane(inner[j * total : (j + 1) * total], e, width) for j in range(res)], axis=1)
                for e in range(share)
            ],
            axis=0,
        )
        parts.append(split(turned * (1.0 / seqs_all)))
    join = lambda pairs, axis: tuple(jnp.concatenate([pair[h] for pair in pairs], axis=axis) for h in (0, 1))
    grad_right[...] = dot3(join(lefts, 1), join(parts, 0), NN)
    spread = tuple(
        jnp.concatenate(
            [jnp.concatenate([x if b == cb else blank for b in range(n)], axis=0) for cb in range(n)], axis=1
        )
        for x in own
    )
    gl = dot3(join(parts, 1), spread, NT)
    for b in range(n):
        for e in range(share):
            row = (e * n + b) * res
            pieces[b, e * res : (e + 1) * res] = gl[row : row + res]
    half = res * share
    keep[:half] = pieces[k]
    keep[half:] = pieces[k ^ 2]
    send[:half] = pieces[k ^ 1]
    send[half:] = pieces[k ^ 3]


def right_of(refs, seqs, tiles, scale):
    rows = [jnp.concatenate([ref[t * seqs : (t + 1) * seqs] for t in range(tiles)], axis=1) for ref in refs]
    return split(jnp.concatenate(rows, axis=0) * scale)


def turn(n, refs, res, share):
    wide = LANES // n
    out = {}
    for e in range(share):
        regs = [ref[pl.ds(e, res, stride=share), :] for ref in refs]
        for b in range(n):
            out[e, b] = jnp.concatenate([lane(reg, b, wide) for reg in regs], axis=1)
    return out


def share_term(n, refs, shares, cot):
    share = res = SUBLANES
    width = seqs = LANES // n
    total = n * res
    tiles = res * width // LANES
    gather_cot(refs, cot, tiles * seqs, res)
    scaled = right_of(refs, seqs, tiles, 1.0 / (n * seqs))
    turned = dot3(scaled, shares, TT)
    stacked = jnp.concatenate(
        [
            jnp.concatenate([lane(turned[j * width : (j + 1) * width], e, total) for j in range(res)], axis=1)
            for e in range(share)
        ],
        axis=0,
    )
    return dot3(split(stacked), split(cot[...].reshape(res * total, LANES)), NN)


def share_kernel(n, r0, r1, r2, r3, own_x, xr, qa, qb, part, cot, both):
    share = res = SUBLANES
    rows = r0.shape[0]
    theirs = turn(n, chosen(n, 1, qa, qb, both), res, share)
    shares = split(jnp.concatenate([theirs[e, b] for e in range(share) for b in range(n)], axis=0))
    far = (own_x.at[own_x.shape[0] - rows :], r1.at[rows:], xr.at[:rows], xr.at[rows:])
    term = share_term(n, (r0, r1, r2, r3), shares, cot.at[0])
    part[...] = term + share_term(n, far, shares, cot.at[1])


def pair_kernel(n, r0, r1, r2, r3, qa, qb, weight, bias, right_flat, pair, grad_right, both):
    share = res = SUBLANES
    width = seqs = LANES // n
    tiles = res * width // LANES
    scaled = right_of((r0, r1, r2, r3), seqs, tiles, 1.0 / (n * seqs))
    mine = turn(n, chosen(n, 0, qa, qb, both), res, share)
    lefts = jnp.concatenate([mine[c % share, c // share] for c in range(width)], axis=0)
    outer = dot3(split(lefts), scaled, NN)
    wide_rows = jnp.concatenate(
        [
            jnp.concatenate([lane(outer[c * res : (c + 1) * res], j, width) for c in range(width)], axis=1)
            for j in range(res)
        ],
        axis=0,
    )
    product = dot3(split(wide_rows), split(weight[...]), NN) + bias[...]
    for j in range(res):
        pair[:, j, :] = product[j * res : (j + 1) * res]
        grad_right[:, j, :] = lane(right_flat, j, width)


def middle_kernel(keep, gl_in, own, out):
    half = keep.shape[0] // 2
    own[...] = keep[:half] + gl_in[:half]
    out[...] = keep[half:] + gl_in[half:]


def last_kernel(
    n, part, part_in, own, gl_in, pair_near, right_near, grad_left, grad_weight, pair, grad_right, left, summed, sem
):
    moves = [(right_near, grad_right), (pair_near, pair), (summed, grad_weight), (left, grad_left)]
    copies = [pltpu.make_async_copy(a, b, sem.at[i]) for i, (a, b) in enumerate(moves)]
    copies[0].start()
    copies[1].start()
    seqs, res, width = left.shape
    share = width // n
    summed[...] = part[...] + part_in[...]
    copies[2].start()
    total = own[...] + gl_in[...]
    for i in range(res):
        picked = jnp.concatenate([total[e * res + i : e * res + i + 1] for e in range(share)], axis=0)
        stacked = jnp.concatenate([lane(picked, cb, seqs) for cb in range(n)], axis=0)
        left[:, i, :] = jnp.transpose(stacked)
    copies[3].start()
    for copy in copies:
        copy.wait()


def swap(x, axis, n, m):
    return lax.ppermute(x, axis, [(a, a ^ m) for a in range(n)])


def shards_packed(n, left_act, right_act, weight, bias, cotangent):
    f32 = jnp.float32
    seqs, res, width = left_act.shape
    pair_width = weight.shape[1]
    rows = seqs * res * width // LANES
    total = n * res
    vmem = pl.BlockSpec(memory_space=pltpu.VMEM)
    shape = lambda *dims: pltpu.VMEM(dims, f32)
    result = lambda *dims: jax.ShapeDtypeStruct(dims, f32)

    def call(kernel, outs, scratch, *args, place=True, out_specs=None):
        spec = vmem if place else pl.BlockSpec(memory_space=pl.ANY)
        if place:
            args = [pltpu.with_memory_space_constraint(a, pltpu.VMEM) for a in args]
        return pl.pallas_call(
            kernel,
            out_shape=outs,
            in_specs=[spec] * len(args),
            out_specs=out_specs or jax.tree.map(lambda _: vmem, outs),
            scratch_shapes=scratch,
        )(*args)

    bias_row = bias.reshape(1, -1)
    lt, rc, own, weight_near, bias_near = call(
        functools.partial(pack_kernel, n),
        (
            shape(rows, LANES),
            shape(2 * rows, LANES),
            shape(3 * rows, LANES),
            shape(*weight.shape),
            shape(*bias_row.shape),
        ),
        [
            pltpu.VMEM(left_act.shape, f32),
            pltpu.VMEM(right_act.shape, f32),
            pltpu.VMEM(cotangent.shape, f32),
            pltpu.SemaphoreType.DMA((2 * n + 3,)),
        ],
        left_act,
        right_act,
        cotangent,
        weight,
        bias_row,
        place=False,
    )
    own_x = swap(own, "col", n, 2)
    far_rows = [swap(rc, "row", n, m) for m in (2, 3)]
    lefts, others = call(join_kernel, (shape(2 * rows, LANES), shape(4 * rows, LANES)), [], lt, rc, own_x)
    next_row = swap(others, "row", n, 1)
    rcs = [rc, next_row] + far_rows
    lts = (lefts, swap(lefts, "col", n, 1))
    cut = call(
        functools.partial(slice_kernel, n), (shape(rows, LANES),) * n, [pltpu.VMEM((2, n, rows, LANES), f32)], *lts
    )
    moved = [cut[0]] + [swap(cut[m], "row", n, m) for m in (1, 2, 3)]
    slices = call(stack_kernel, shape(n * rows, LANES), [], *moved)
    qs = (slices, swap(slices, "col", n, 1))
    both_scratch = pltpu.VMEM((2, n * rows, LANES), f32)
    stacked = call(stack_kernel, shape(4 * rows, LANES), [], *far_rows)
    xr = swap(stacked, "col", n, 2)
    cot_scratch = pltpu.VMEM((res, total, pair_width), f32)
    right_flat, keep, send = call(
        functools.partial(grads_kernel, n, n * seqs),
        (shape(seqs, res * width), shape(2 * rows, LANES), shape(2 * rows, LANES)),
        [
            pltpu.VMEM((n * rows, LANES), f32),
            cot_scratch,
            pltpu.VMEM((n, rows, LANES), f32),
        ],
        *lts,
        *rcs,
        weight_near,
    )
    gl_c = swap(send, "col", n, 1)
    own_gl, out = call(middle_kernel, (shape(rows, LANES), shape(rows, LANES)), [], keep, gl_c)
    gl_x = swap(out, "col", n, 2)
    pair, grad_right = call(
        functools.partial(pair_kernel, n),
        (shape(res, res, pair_width), shape(seqs, res, width)),
        [both_scratch],
        *rcs,
        *qs,
        weight_near,
        bias_near,
        right_flat,
    )
    own_rows = width * width // n
    part = call(
        functools.partial(share_kernel, n),
        shape(own_rows, pair_width),
        [pltpu.VMEM((2, res, total, pair_width), f32), both_scratch],
        *rcs,
        own_x,
        xr,
        *qs,
    )
    part_in = swap(part, "col", n, 1)
    grad_left, grad_weight, pair, grad_right = call(
        functools.partial(last_kernel, n),
        (
            result(seqs, res, width),
            result(own_rows, pair_width),
            result(res, res, pair_width),
            result(seqs, res, width),
        ),
        [
            pltpu.VMEM((seqs, res, width), f32),
            pltpu.VMEM((own_rows, pair_width), f32),
            pltpu.SemaphoreType.DMA((4,)),
        ],
        part,
        part_in,
        own_gl,
        gl_x,
        pair,
        grad_right,
        out_specs=(pl.BlockSpec(memory_space=pl.ANY),) * 4,
    )
    return (pair, grad_left, grad_right, grad_weight)


def packs(mesh, n, left_act, weight, cotangent):
    seqs, res, width = left_act.shape
    return (
        n == 4
        and mesh.shape["col"] == n
        and cotangent.shape[:2] == (res, res)
        and n * seqs == n * width == weight.shape[1] == LANES
        and res == width // n == SUBLANES
    )


def solution(mesh):
    placed = (
        P(("groups", "row"), "col", None),
        P(("groups", "row"), "col", None),
        P(),
        P(),
        P(("groups", "row"), "col", None),
    )
    n = mesh.shape["row"]

    def shards(left_act, right_act, weight, bias, cotangent):
        if packs(mesh, n, left_act, weight, cotangent):
            return shards_packed(n, left_act, right_act, weight, bias, cotangent)
        return shards_general(left_act, right_act, weight, bias, cotangent)

    return jax.shard_map(
        shards,
        mesh=mesh,
        in_specs=placed,
        out_specs=(
            P(("groups", "row"), "col", None),
            P(("groups", "row"), "col", None),
            P(("groups", "row"), "col", None),
            P(("groups", "row"), None),
        ),
        check_vma=False,
    )
```

```python
import functools

import jax
import jax.numpy as jnp
from jax import lax
from jax.experimental import pallas as pl
from jax.experimental.pallas import tpu as pltpu
from jax.sharding import PartitionSpec as P


LANES, SUBLANES = 128, 8
NT = (((1,), (1,)), ((), ()))
NN = (((1,), (0,)), ((), ()))
TN = (((0,), (0,)), ((), ()))
TT = (((0,), (1,)), ((), ()))


def block_terms(left_block, right_full, cot_block, weight_cube, bias):
    seqs = right_full.shape[0]
    highest = lax.Precision.HIGHEST
    products = jnp.einsum("sic,sjd->icjd", left_block, right_full, precision=highest) / seqs
    pair_block = jnp.einsum("icjd,cdz->ijz", products, weight_cube, precision=highest) + bias
    grad_outer = jnp.einsum("ijz,cdz->icjd", cot_block, weight_cube, precision=highest)
    weight_term = jnp.einsum("icjd,ijz->cdz", products, cot_block, precision=highest)
    left_term = jnp.einsum("icjd,sjd->sic", grad_outer, right_full, precision=highest) / seqs
    right_term = jnp.einsum("icjd,sic->sjd", grad_outer, left_block, precision=highest) / seqs
    return (pair_block, weight_term, left_term, right_term)


def shards_general(left_act, right_act, weight, bias, cotangent):
    width = left_act.shape[2]
    pair_width = weight.shape[1]
    widened = lax.all_gather(left_act, "col", axis=1, tiled=True)
    left_full = lax.all_to_all(widened, "row", split_axis=1, concat_axis=0, tiled=True)
    right_full = lax.all_gather(right_act, "row", axis=0, tiled=True)
    weight_cube = weight.reshape(width, width, pair_width)
    pair, grad_cube, left_partial, right_partial = block_terms(
        left_full, right_full, cotangent, weight_cube, bias
    )
    returned = lax.all_to_all(left_partial, "row", split_axis=0, concat_axis=1, tiled=True)
    grad_left = lax.psum_scatter(returned, "col", scatter_dimension=1, tiled=True)
    grad_right = lax.psum_scatter(right_partial, "row", scatter_dimension=0, tiled=True)
    grad_flat = grad_cube.reshape(width * width, pair_width)
    weight_part = lax.psum_scatter(grad_flat, "row", scatter_dimension=0, tiled=True)
    grad_weight = lax.psum(weight_part, "col")
    return (pair, grad_left, grad_right, grad_weight)


def split(x):
    hi = x.astype(jnp.bfloat16)
    return hi, (x - hi.astype(jnp.float32)).astype(jnp.bfloat16)


def dot3(a, b, dims):
    dot = functools.partial(lax.dot_general, dimension_numbers=dims, preferred_element_type=jnp.float32)
    (ah, al), (bh, bl) = a, b
    return dot(ah, bh) + (dot(ah, bl) + dot(al, bh))


def lane(x, block, width):
    return x[:, block * width : (block + 1) * width]


def pack_kernel(n, left, right, cot, weight, bias, lt, rc, own, weight_out, bias_out, lv, rv, cv, sem):
    moves = [(left, lv), (right, rv), (cot, cv), (weight, weight_out), (bias, bias_out)]
    copies = [pltpu.make_async_copy(a, b, sem.at[i]) for i, (a, b) in enumerate(moves)]
    for copy in copies:
        copy.start()
    seqs, res, width = lv.shape
    share = width // n
    copies[0].wait()
    flat = jnp.concatenate([lv[:, i, :] for i in range(res)], axis=1)
    turned = jnp.transpose(flat)
    for i in range(res):
        rows = [turned[(i * n + b) * share : (i * n + b + 1) * share] for b in range(n)]
        lt[i * share : (i + 1) * share] = jnp.concatenate(rows, axis=1)
    per = LANES // width
    tiles = res // per
    copies[1].wait()
    for t in range(tiles):
        rc[t * seqs : (t + 1) * seqs] = jnp.concatenate([rv[:, t * per + j, :] for j in range(per)], axis=1)
    base = tiles * seqs
    copies[2].wait()
    for j in range(cv.shape[1]):
        rc[base + j * res : base + (j + 1) * res] = cv[:, j, :]
    own[: lt.shape[0]] = lt[...]
    own[lt.shape[0] :] = rc[...]
    copies[3].wait()
    copies[4].wait()


def slice_kernel(n, l0, l1, l2, l3, p0, p1, p2, p3, held, built):
    r, k = lax.axis_index("row"), lax.axis_index("col")
    rows = l0.shape[0]
    wide = LANES // n
    for m, ref in enumerate((l0, l1, l2, l3)):
        held[k ^ m] = ref[:rows]
    owner = lax.broadcasted_iota(jnp.int32, (rows, LANES), 1) // wide
    for dest in range(n):
        out = None
        for b in range(n):
            block = held[b]
            shift = ((b - dest) * wide) % LANES
            if shift:
                block = pltpu.roll(block, shift, 1)
            out = block if out is None else jnp.where(owner == b, block, out)
        built[dest] = out
    for m, ref in enumerate((p0, p1, p2, p3)):
        ref[:rows] = held[r ^ m]
        ref[rows:] = built[r ^ m]


def stack_kernel(r1, r2, r3, out):
    rows = r1.shape[0]
    for m, ref in enumerate((r1, r2, r3)):
        out[m * rows : (m + 1) * rows] = ref[...]


def gather_cot(rcs, cot, base, res):
    r = lax.axis_index("row")
    for m, ref in enumerate(rcs):
        for j in range(res):
            cot[j, pl.ds(pl.multiple_of((r ^ m) * res, res), res), :] = ref[base + j * res : base + (j + 1) * res]


def grads_kernel(n, seqs_all, l0, l1, l2, l3, r0, r1, r2, r3, weight, grad_right, keep, send, held, cot, inner, pieces):
    k = lax.axis_index("col")
    seqs, res, width = grad_right.shape
    share = width // n
    wide = LANES // n
    total = n * res
    tiles = res * width // LANES
    base = tiles * seqs
    for m, ref in enumerate((l0, l1, l2, l3)):
        held[pl.ds((k ^ m) * res * share, res * share)] = ref[: res * share]
    gather_cot((r0, r1, r2, r3), cot, base, res)
    cots = split(cot[...].reshape(res * total, LANES))
    inner[...] = dot3(cots, split(weight[...]), NT)
    turned = jnp.concatenate(
        [
            jnp.concatenate(
                [inner[j * total : (j + 1) * total, c * width : (c + 1) * width] for j in range(res)], axis=1
            )
            for c in range(width)
        ],
        axis=0,
    )
    g = split(turned * (1.0 / seqs_all))
    by_share = [held[pl.ds(e, total, stride=share), :] for e in range(share)]
    left = jnp.concatenate([lane(by_share[c % share], c // share, wide) for c in range(width)], axis=0)
    gr = dot3(split(left), g, TN)
    for j in range(res):
        grad_right[:, j, :] = lane(gr, j, width)
    own = jnp.concatenate([r0[t * seqs : (t + 1) * seqs] for t in range(tiles)], axis=1)
    gl = dot3(g, split(own), NT)
    for b in range(n):
        for e in range(share):
            parts = []
            for cb in range(n):
                row = ((cb * share + e) * n + b) * res
                parts.append(gl[row : row + res])
            pieces[b, e * res : (e + 1) * res] = jnp.concatenate(parts, axis=1)
    half = res * share
    keep[:half] = pieces[k]
    keep[half:] = pieces[k ^ 2]
    send[:half] = pieces[k ^ 1]
    send[half:] = pieces[k ^ 3]


def right_of(refs, seqs, tiles, scale):
    rows = [jnp.concatenate([ref[t * seqs : (t + 1) * seqs] for t in range(tiles)], axis=1) for ref in refs]
    return split(jnp.concatenate(rows, axis=0) * scale)


def turn(n, refs, offset, res, share):
    wide = LANES // n
    out = {}
    for e in range(share):
        regs = [ref[pl.ds(offset + e, res, stride=share), :] for ref in refs]
        for b in range(n):
            out[e, b] = jnp.concatenate([lane(reg, b, wide) for reg in regs], axis=1)
    return out


def share_kernel(n, r0, r1, r2, r3, own_x, xr, q0, q1, q2, q3, part, cot):
    share = res = SUBLANES
    rows = r0.shape[0]
    rx = [own_x.at[own_x.shape[0] - rows :]] + [xr.at[m * rows : (m + 1) * rows] for m in range(n - 1)]
    width = seqs = LANES // n
    total = n * res
    tiles = res * width // LANES
    theirs = turn(n, (q0, q1, q2, q3), res * share, res, share)
    shares = split(jnp.concatenate([theirs[e, b] for e in range(share) for b in range(n)], axis=0))
    terms = None
    for refs in ((r0, r1, r2, r3), rx):
        gather_cot(refs, cot, tiles * seqs, res)
        scaled = right_of(refs, seqs, tiles, 1.0 / (n * seqs))
        turned = dot3(scaled, shares, TT)
        stacked = jnp.concatenate(
            [
                jnp.concatenate([lane(turned[j * width : (j + 1) * width], e, total) for j in range(res)], axis=1)
                for e in range(share)
            ],
            axis=0,
        )
        term = dot3(split(stacked), split(cot[...].reshape(res * total, LANES)), NN)
        terms = term if terms is None else terms + term
    part[...] = terms


def pair_kernel(n, r0, r1, r2, r3, q0, q1, q2, q3, weight, bias, pair):
    share = res = SUBLANES
    width = seqs = LANES // n
    tiles = res * width // LANES
    scaled = right_of((r0, r1, r2, r3), seqs, tiles, 1.0 / (n * seqs))
    mine = turn(n, (q0, q1, q2, q3), 0, res, share)
    lefts = jnp.concatenate([mine[c % share, c // share] for c in range(width)], axis=0)
    outer = dot3(split(lefts), scaled, NN)
    wide_rows = jnp.concatenate(
        [
            jnp.concatenate([lane(outer[c * res : (c + 1) * res], j, width) for c in range(width)], axis=1)
            for j in range(res)
        ],
        axis=0,
    )
    product = dot3(split(wide_rows), split(weight[...]), NN) + bias[...]
    for j in range(res):
        pair[:, j, :] = product[j * res : (j + 1) * res]


def middle_kernel(keep, gl_in, own, out):
    half = keep.shape[0] // 2
    own[...] = keep[:half] + gl_in[:half]
    out[...] = keep[half:] + gl_in[half:]


def last_kernel(n, part, part_in, own, gl_in, grad_left, grad_weight):
    seqs, res, width = grad_left.shape
    share = width // n
    grad_weight[...] = part[...] + part_in[...]
    total = own[...] + gl_in[...]
    for i in range(res):
        picked = jnp.concatenate([total[e * res + i : e * res + i + 1] for e in range(share)], axis=0)
        stacked = jnp.concatenate([lane(picked, cb, seqs) for cb in range(n)], axis=0)
        grad_left[:, i, :] = jnp.transpose(stacked)


def swap(x, axis, n, m):
    return lax.ppermute(x, axis, [(a, a ^ m) for a in range(n)])


def shards_packed(n, left_act, right_act, weight, bias, cotangent):
    f32 = jnp.float32
    seqs, res, width = left_act.shape
    pair_width = weight.shape[1]
    rows = seqs * res * width // LANES
    total = n * res
    vmem = pl.BlockSpec(memory_space=pltpu.VMEM)
    shape = lambda *dims: pltpu.VMEM(dims, f32)
    result = lambda *dims: jax.ShapeDtypeStruct(dims, f32)

    def call(kernel, outs, scratch, *args, place=True):
        spec = vmem if place else pl.BlockSpec(memory_space=pl.ANY)
        if place:
            args = [pltpu.with_memory_space_constraint(a, pltpu.VMEM) for a in args]
        return pl.pallas_call(
            kernel,
            out_shape=outs,
            in_specs=[spec] * len(args),
            out_specs=jax.tree.map(lambda _: vmem, outs),
            scratch_shapes=scratch,
        )(*args)

    bias_row = bias.reshape(1, -1)
    lt, rc, own, weight_near, bias_near = call(
        functools.partial(pack_kernel, n),
        (
            shape(rows, LANES),
            shape(2 * rows, LANES),
            shape(3 * rows, LANES),
            shape(*weight.shape),
            shape(*bias_row.shape),
        ),
        [
            pltpu.VMEM(left_act.shape, f32),
            pltpu.VMEM(right_act.shape, f32),
            pltpu.VMEM(cotangent.shape, f32),
            pltpu.SemaphoreType.DMA((5,)),
        ],
        left_act,
        right_act,
        cotangent,
        weight,
        bias_row,
        place=False,
    )
    own_x = swap(own, "col", n, 2)
    rcs = [rc] + [swap(rc, "row", n, m) for m in (1, 2, 3)]
    lt_c = swap(lt, "col", n, 1)
    own_xc = swap(own_x, "col", n, 1)
    lts = (lt, lt_c, own_x, own_xc)
    cut = call(
        functools.partial(slice_kernel, n), (shape(2 * rows, LANES),) * n, [pltpu.VMEM((n, rows, LANES), f32)] * 2, *lts
    )
    qs = [cut[0]] + [swap(cut[m], "row", n, m) for m in (1, 2, 3)]
    stacked = call(stack_kernel, shape((n - 1) * 2 * rows, LANES), [], *rcs[1:])
    xr = swap(stacked, "col", n, 2)
    cot_scratch = pltpu.VMEM((res, total, pair_width), f32)
    grad_right, keep, send = call(
        functools.partial(grads_kernel, n, n * seqs),
        (result(seqs, res, width), shape(2 * rows, LANES), shape(2 * rows, LANES)),
        [
            pltpu.VMEM((n * rows, LANES), f32),
            cot_scratch,
            pltpu.VMEM((res * total, width * width), f32),
            pltpu.VMEM((n, rows, LANES), f32),
        ],
        *lts,
        *rcs,
        weight_near,
    )
    gl_c = swap(send, "col", n, 1)
    own_gl, out = call(middle_kernel, (shape(rows, LANES), shape(rows, LANES)), [], keep, gl_c)
    gl_x = swap(out, "col", n, 2)
    pair = call(functools.partial(pair_kernel, n), result(res, res, pair_width), [], *rcs, *qs, weight_near, bias_near)
    own_rows = width * width // n
    part = call(functools.partial(share_kernel, n), shape(own_rows, pair_width), [cot_scratch], *rcs, own_x, xr, *qs)
    part_in = swap(part, "col", n, 1)
    grad_left, grad_weight = call(
        functools.partial(last_kernel, n),
        (result(seqs, res, width), result(own_rows, pair_width)),
        [],
        part,
        part_in,
        own_gl,
        gl_x,
    )
    return (pair, grad_left, grad_right, grad_weight)


def packs(mesh, n, left_act, weight, cotangent):
    seqs, res, width = left_act.shape
    return (
        n == 4
        and mesh.shape["col"] == n
        and cotangent.shape[:2] == (res, res)
        and n * seqs == n * width == weight.shape[1] == LANES
        and res == width // n == SUBLANES
    )


def solution(mesh):
    placed = (
        P(("groups", "row"), "col", None),
        P(("groups", "row"), "col", None),
        P(),
        P(),
        P(("groups", "row"), "col", None),
    )
    n = mesh.shape["row"]

    def shards(left_act, right_act, weight, bias, cotangent):
        if packs(mesh, n, left_act, weight, cotangent):
            return shards_packed(n, left_act, right_act, weight, bias, cotangent)
        return shards_general(left_act, right_act, weight, bias, cotangent)

    return jax.shard_map(
        shards,
        mesh=mesh,
        in_specs=placed,
        out_specs=(
            P(("groups", "row"), "col", None),
            P(("groups", "row"), "col", None),
            P(("groups", "row"), "col", None),
            P(("groups", "row"), None),
        ),
        check_vma=False,
    )
```
